32 devices in a mesh: fsdp: 8 (over y, x, core), sp: 4 (over z).
Axes of the slice: x: 2, y: 2, z: 4, core: 2. Of those that a mesh axis runs over, the one named last changes fastest.
Arguments:
- block_input: float32 [4096, 2048], P(('fsdp', 'sp')), may hold values from -6 to 6
- out_grad: float32 [4096, 2048], P(('fsdp', 'sp')), may hold values from -6 to 6
- qkvg_weight: bfloat16 [2048, 12288], P(('fsdp', 'sp')), may hold values from -0.125 to 0.125
- out_weight: bfloat16 [4096, 2048], P(('fsdp', 'sp')), may hold values from -0.125 to 0.125
- mlp_in_weight: bfloat16 [2048, 8192], P(('fsdp', 'sp')), may hold values from -0.125 to 0.125
- mlp_out_weight: bfloat16 [4096, 2048], P(('fsdp', 'sp')), may hold values from -0.125 to 0.125
- norm_gains: bfloat16 [2, 2048], P(None, ('fsdp', 'sp')), may hold values from 0.099609375 to 1.8984375
- group_gain: bfloat16 [4096], P(('fsdp', 'sp')), may hold values from 0.099609375 to 1.8984375
- decay_rate: float32 [8], replicated, may hold values from 7.324219e-05 to 0.04, as said below
Outputs:
- block_output: float32 [4096, 2048], P(('fsdp', 'sp'))
- input_grad: float32 [4096, 2048], P(('fsdp', 'sp'))
- qkvg_grad: float32 [2048, 12288], P(('fsdp', 'sp'))
- out_weight_grad: float32 [4096, 2048], P(('fsdp', 'sp'))
- mlp_in_grad: float32 [2048, 8192], P(('fsdp', 'sp'))
- mlp_out_grad: float32 [4096, 2048], P(('fsdp', 'sp'))
- norm_gains_grad: float32 [2, 2048], P(None, ('fsdp', 'sp'))
- group_gain_grad: float32 [4096], P(('fsdp', 'sp'))
The draws below stay inside these ranges and needn't reach their ends.
Inputs may be any that keep to these rules, and one draw needn't show every extreme that they name: `decay_rate`: each head's rate holds for the whole run.
All inputs are finite; a program needn't handle non-finite values.
Results may differ from the reference program's by a relative error of at most 0.025.
Values may be sent and summed in bfloat16 or wider, within the bound.
No kernel may reach another device: no remote copies, remote signals or barrier semaphores. Data moves between devices by JAX's collectives and lax.ppermute only.
A program may use at most 192 MiB of HBM per device.

```python
import math
import jax
import jax.numpy as jnp
from jax import lax

D = 2048
HEADS = 8
KEY = 256
VAL = 512
FF = 4096
SEQS = 1
BLOCK = 512
TOKENS = 4096
SEQ_LEN = 4096
QKVG = 12288


def draw_decay_rate(key, part):
    ranking = jax.random.permutation(jax.random.fold_in(key, 11), jnp.arange(HEADS))
    slow_rate = jnp.exp(jax.random.uniform(jax.random.fold_in(key, 12), (HEADS,), jnp.float32, math.log(0.3), math.log(2.0))) / SEQ_LEN
    fast_rate = 1.0 / jax.random.uniform(jax.random.fold_in(key, 13), (HEADS,), jnp.float32, 25.0, 50.0)
    slow_count = HEADS // 2
    return jnp.where(ranking < slow_count, slow_rate, fast_rate)


def block_levels(stream_key, dims, cuts, smallest, top_value):
    factor_of, own = 1.0, jax.random.fold_in(stream_key, 6)
    for position, parts in cuts:
        steps = jnp.exp(jax.random.uniform(jax.random.fold_in(own, position), (parts,), jnp.float32, smallest / len(cuts), top_value / len(cuts)))
        factor_of = factor_of * jnp.repeat(steps, dims[position] // parts).reshape([-1 if axis == position else 1 for axis in range(len(dims))])
    return factor_of


def scatter_about(stream_key, dims, width, bound, shards=(), kind=jnp.bfloat16):
    gain = block_levels(stream_key, dims, shards, -0.22, 0.18) if shards else 1.0
    values = jax.random.normal(stream_key, dims, jnp.float32) * width * gain
    return jnp.minimum(jnp.maximum(values, -bound), bound).astype(kind)


def setup_inputs(seed: int = 0) -> dict:
    seeds = jax.random.split(jax.random.key(seed), 10)
    block_input = scatter_about(seeds[0], (TOKENS, D), 1.0, 6.0, ((0, 32),), jnp.float32)
    out_grad = scatter_about(seeds[1], (TOKENS, D), 1.0, 6.0, ((0, 32),), jnp.float32)
    qkvg_weight = scatter_about(seeds[2], (D, QKVG), D ** -0.5, 0.125, ((0, 32),))
    out_weight = scatter_about(seeds[3], (HEADS * VAL, D), (HEADS * VAL // 2) ** -0.5, 0.125, ((0, 32),))
    mlp_in_weight = scatter_about(seeds[4], (D, 2 * FF), D ** -0.5, 0.125, ((0, 32),))
    mlp_out_weight = scatter_about(seeds[5], (FF, D), (FF // 2) ** -0.5, 0.125, ((0, 32),))
    norm_gains = jnp.clip(1.0 + 0.18 * jax.random.normal(seeds[6], (2, D), jnp.float32), 0.099609375, 1.8984375).astype(jnp.bfloat16)
    group_gain = jnp.clip(1.0 + 0.18 * jax.random.normal(seeds[7], (HEADS * VAL,), jnp.float32), 0.099609375, 1.8984375).astype(jnp.bfloat16)
    decay_rate = draw_decay_rate(jax.random.fold_in(seeds[9], 71), 0)
    return {"block_input": block_input, "out_grad": out_grad, "qkvg_weight": qkvg_weight, "out_weight": out_weight, "mlp_in_weight": mlp_in_weight, "mlp_out_weight": mlp_out_weight, "norm_gains": norm_gains, "group_gain": group_gain, "decay_rate": decay_rate}


epsilon = 1e-05

def rounded(value):
    return lax.optimization_barrier(value.astype(jnp.bfloat16)).astype(jnp.float32)

def layer_norm(values):
    average = lax.optimization_barrier(jnp.mean(values, axis=-1, keepdims=True))
    centered = values - average
    inv_std = lax.rsqrt(lax.optimization_barrier(jnp.mean(centered * centered, axis=-1, keepdims=True)) + epsilon)
    return (centered * inv_std, inv_std)

def norm_back(upstream, normed, inv_std):
    return inv_std * (upstream - lax.optimization_barrier(jnp.mean(upstream, axis=-1, keepdims=True)) - normed * lax.optimization_barrier(jnp.mean(upstream * normed, axis=-1, keepdims=True)))

def gelu_parts(inputs):
    normal_cdf = 0.5 * (1.0 + lax.erf(inputs * 0.7071067811865476))
    return (inputs * normal_cdf, normal_cdf + inputs * jnp.exp(-0.5 * inputs * inputs) * 0.3989422804014327)

def decay_tables(decays, length):
    offsets = jnp.arange(length, dtype=jnp.float32)
    spread = offsets[:, None] - offsets[None, :]
    within = jnp.where(spread[None] >= 0.0, jnp.exp(-decays[:, None, None] * jnp.maximum(spread, 0.0)[None]), 0.0)
    query_decay = jnp.exp(-decays[None, :] * (offsets[:, None] + 1.0))
    key_decay = jnp.exp(-decays[None, :] * (length - 1.0 - offsets[:, None]))
    per_block = jnp.exp(-decays * length)
    return (within, query_decay, key_decay, per_block)

def reference(block_input, out_grad, qkvg_weight, out_weight, mlp_in_weight, mlp_out_weight, norm_gains, group_gain, decay_rate):
    key_cols = HEADS * KEY
    value_cols = HEADS * VAL
    key_scale = KEY ** (-0.5)
    block_count = SEQ_LEN // BLOCK
    within, query_decay, key_decay, per_block = decay_tables(decay_rate, BLOCK)
    gain_one = norm_gains[0].astype(jnp.float32)
    gain_two = norm_gains[1].astype(jnp.float32)
    gain_group = group_gain.astype(jnp.float32)
    zero_state = jnp.zeros((HEADS, KEY, VAL), jnp.float32)

    def one_sequence(totals, pieces):
        inputs, upstream = pieces
        normed_one, inv_one = layer_norm(inputs)
        hidden_one = (normed_one * gain_one).astype(jnp.bfloat16)
        projected = jnp.dot(hidden_one, qkvg_weight, preferred_element_type=jnp.float32)
        query_f = rounded(projected[:, :key_cols] * key_scale).reshape(block_count, BLOCK, HEADS, KEY)
        key_f = rounded(projected[:, key_cols:2 * key_cols]).reshape(block_count, BLOCK, HEADS, KEY)
        value_f = rounded(projected[:, 2 * key_cols:2 * key_cols + value_cols]).reshape(block_count, BLOCK, HEADS, VAL)
        gate_values = projected[:, 2 * key_cols + value_cols:]
        scores = rounded(jnp.einsum('nihk,njhk->nhij', query_f, key_f) * within[None])
        intra_part = jnp.einsum('nhij,njhv->nihv', scores, value_f)
        query_scaled = rounded(query_f * query_decay[None, :, :, None])
        key_scaled = rounded(key_f * key_decay[None, :, :, None])
        updates = jnp.einsum('nihk,nihv->nhkv', key_scaled, value_f)

        def advance(running, block_update):
            return (per_block[:, None, None] * running + block_update, running)
        _, earlier = lax.scan(advance, zero_state, updates)
        state_rounded = rounded(earlier)
        retained = intra_part + jnp.einsum('nihk,nhkv->nihv', query_scaled, state_rounded)
        group_normed, group_inv = layer_norm(retained.reshape(SEQ_LEN, HEADS, VAL))
        group_sent = rounded(group_normed).reshape(SEQ_LEN, value_cols)
        sigmoid_gate = jax.nn.sigmoid(gate_values)
        swish_gate = gate_values * sigmoid_gate
        mixed_heads = (gain_group * group_sent * swish_gate).astype(jnp.bfloat16)
        middle = inputs + jnp.dot(mixed_heads, out_weight, preferred_element_type=jnp.float32)
        normed_two, inv_two = layer_norm(middle)
        hidden_two = (normed_two * gain_two).astype(jnp.bfloat16)
        inner_proj = jnp.dot(hidden_two, mlp_in_weight, preferred_element_type=jnp.float32)
        activated, gelu_slope = gelu_parts(inner_proj[:, :FF])
        up_part = inner_proj[:, FF:]
        product = (activated * up_part).astype(jnp.bfloat16)
        output = middle + jnp.dot(product, mlp_out_weight, preferred_element_type=jnp.float32)
        out_rounded = upstream.astype(jnp.bfloat16)
        down_term = jnp.dot(product.T, out_rounded, preferred_element_type=jnp.float32)
        grad_product = jnp.dot(out_rounded, mlp_out_weight.T, preferred_element_type=jnp.float32)
        grad_inner = jnp.concatenate([grad_product * up_part * gelu_slope, grad_product * activated], axis=1).astype(jnp.bfloat16)
        in_term = jnp.dot(hidden_two.T, grad_inner, preferred_element_type=jnp.float32)
        grad_hidden_two = jnp.dot(grad_inner, mlp_in_weight.T, preferred_element_type=jnp.float32)
        gain_two_term = lax.optimization_barrier(jnp.sum(grad_hidden_two * normed_two, axis=0))
        grad_middle = upstream + norm_back(grad_hidden_two * gain_two, normed_two, inv_two)
        middle_rounded = grad_middle.astype(jnp.bfloat16)
        out_term = jnp.dot(mixed_heads.T, middle_rounded, preferred_element_type=jnp.float32)
        grad_mixed = jnp.dot(middle_rounded, out_weight.T, preferred_element_type=jnp.float32)
        group_term = lax.optimization_barrier(jnp.sum(grad_mixed * group_sent * swish_gate, axis=0))
        grad_group = rounded(grad_mixed * gain_group * swish_gate).reshape(SEQ_LEN, HEADS, VAL)
        grad_gate = grad_mixed * gain_group * group_sent * sigmoid_gate * (1.0 + gate_values * (1.0 - sigmoid_gate))
        grad_retained = rounded(norm_back(grad_group, group_normed, group_inv)).reshape(block_count, BLOCK, HEADS, VAL)
        grad_scores = rounded(jnp.einsum('nihv,njhv->nhij', grad_retained, value_f) * within[None])
        directs = jnp.einsum('nihk,nihv->nhkv', query_scaled, grad_retained)

        def retreat(later_grad, direct_grad):
            return (direct_grad + per_block[:, None, None] * later_grad, later_grad)
        _, afterward = lax.scan(retreat, zero_state, directs, reverse=True)
        later_rounded = rounded(afterward)
        grad_query = (jnp.einsum('nhij,njhk->nihk', grad_scores, key_f) + jnp.einsum('nihv,nhkv->nihk', grad_retained, state_rounded) * query_decay[None, :, :, None]) * key_scale
        grad_key = jnp.einsum('nhij,nihk->njhk', grad_scores, query_f) + jnp.einsum('nihv,nhkv->nihk', value_f, later_rounded) * key_decay[None, :, :, None]
        grad_value = jnp.einsum('nhij,nihv->njhv', scores, grad_retained) + jnp.einsum('nihk,nhkv->nihv', key_scaled, later_rounded)
        grad_projected = jnp.concatenate([grad_query.reshape(SEQ_LEN, key_cols), grad_key.reshape(SEQ_LEN, key_cols), grad_value.reshape(SEQ_LEN, value_cols), grad_gate], axis=1).astype(jnp.bfloat16)
        qkvg_term = jnp.dot(hidden_one.T, grad_projected, preferred_element_type=jnp.float32)
        grad_hidden_one = jnp.dot(grad_projected, qkvg_weight.T, preferred_element_type=jnp.float32)
        gain_one_term = lax.optimization_barrier(jnp.sum(grad_hidden_one * normed_one, axis=0))
        input_grad = grad_middle + norm_back(grad_hidden_one * gain_one, normed_one, inv_one)
        totals = (totals[0] + qkvg_term, totals[1] + out_term, totals[2] + in_term, totals[3] + down_term, totals[4] + jnp.stack([gain_one_term, gain_two_term]), totals[5] + group_term)
        return (totals, (output, input_grad))
    starting = (jnp.zeros((D, QKVG), jnp.float32), jnp.zeros((HEADS * VAL, D), jnp.float32), jnp.zeros((D, 2 * FF), jnp.float32), jnp.zeros((FF, D), jnp.float32), jnp.zeros((2, D), jnp.float32), jnp.zeros((HEADS * VAL,), jnp.float32))
    totals, results = lax.scan(one_sequence, starting, (block_input.reshape(SEQS, SEQ_LEN, D), out_grad.reshape(SEQS, SEQ_LEN, D)))
    block_output = results[0].reshape(TOKENS, D)
    input_grad = results[1].reshape(TOKENS, D)
    return (block_output, input_grad, totals[0], totals[1], totals[2], totals[3], totals[4], totals[5])
```

```python
import jax
import jax.numpy as jnp
from jax import lax
from jax.sharding import Mesh, PartitionSpec as P

D = 2048
HEADS = 8
KEY = 256
VAL = 512
FF = 4096
SEQS = 1
BLOCK = 512

epsilon = 1e-05
CORES = 2
ALL = ("chip", "core", "sp")
bf16 = jnp.bfloat16
f32 = jnp.float32


def layer_norm(values):
    average = jnp.mean(values, axis=-1, keepdims=True)
    centered = values - average
    inv_std = lax.rsqrt(jnp.mean(centered * centered, axis=-1, keepdims=True) + epsilon)
    return (centered * inv_std, inv_std)


def norm_back(upstream, normed, inv_std):
    return inv_std * (
        upstream
        - jnp.mean(upstream, axis=-1, keepdims=True)
        - normed * jnp.mean(upstream * normed, axis=-1, keepdims=True)
    )


def gelu_parts(inputs):
    normal_cdf = 0.5 * (1.0 + lax.erf(inputs * 0.7071067811865476))
    return (
        inputs * normal_cdf,
        normal_cdf + inputs * jnp.exp(-0.5 * inputs * inputs) * 0.3989422804014327,
    )


def shift(value, axis, step):
    count = lax.axis_size(axis)
    return lax.ppermute(value, axis, [(i, (i + step) % count) for i in range(count)])


def put(buffer, value, index):
    return lax.dynamic_update_index_in_dim(buffer, value, index, 0)


def take(buffer, index):
    return lax.dynamic_index_in_dim(buffer, index, 0, False)


class Groups:
    def __init__(self, mesh):
        count = mesh.shape["sp"]
        self.split = HEADS % (CORES * count) == 0
        self.model = ("core", "sp") if self.split else ("sp",)
        self.token = ("chip",) if self.split else ("chip", "core")
        self.sp = count
        self.models = count * (CORES if self.split else 1)
        self.tokens = mesh.size // self.models

    def gather_model(self, value):
        if not self.split:
            return lax.all_gather(value, self.model, axis=0, tiled=True)
        place = lax.axis_index("sp")
        core = lax.axis_index("core")
        buffer = jnp.zeros((CORES * self.sp,) + value.shape, value.dtype)
        for step in range(self.sp):
            got = value if step == 0 else shift(value, "sp", step)
            source = (place - step) % self.sp
            buffer = put(buffer, got, core * self.sp + source)
            other = shift(got, "core", 1)
            buffer = put(buffer, other, (1 - core) * self.sp + source)
        return buffer.reshape((-1,) + value.shape[1:])

    def scatter_model(self, part_of, rows):
        if not self.split:
            whole = part_of(0, rows * self.models)
            return lax.psum_scatter(
                whole.astype(bf16), self.model, scatter_dimension=0, tiled=True
            ).astype(f32)
        place = lax.axis_index("sp")
        core = lax.axis_index("core")
        half = rows * self.sp
        sent = part_of((1 - core) * half, half).astype(bf16)
        came = shift(sent, "core", 1)
        own = part_of(core * half, half) + came.astype(f32)
        own = own.reshape((self.sp, rows) + own.shape[1:])
        own_low = own.astype(bf16)
        total = take(own, place)
        for step in range(1, self.sp):
            got = shift(take(own_low, (place + step) % self.sp), "sp", step)
            total = total + got.astype(f32)
        return total

    def gather_token(self, value):
        return lax.all_gather(value, self.token, axis=0, tiled=True)

    def scatter_token(self, value):
        return lax.psum_scatter(value, self.token, scatter_dimension=0, tiled=True)

    def exchange(self, blocks):
        if not self.split:
            return lax.all_to_all(blocks, self.model, split_axis=0, concat_axis=0, tiled=True)
        mine = lax.axis_index(self.model)
        result = put(jnp.zeros_like(blocks), take(blocks, mine), mine)
        for step in range(1, self.models):
            got = shift(take(blocks, (mine + step) % self.models), self.model, step)
            result = put(result, got, (mine - step) % self.models)
        return result

    def owner_pairs(self):
        return [(d, (d % self.tokens) * self.models + d // self.tokens) for d in range(self.tokens * self.models)]


def decay_tables(decays, length):
    offsets = jnp.arange(length, dtype=f32)
    spread = offsets[:, None] - offsets[None, :]
    within = jnp.where(
        spread[None] >= 0.0, jnp.exp(-decays[:, None, None] * jnp.maximum(spread, 0.0)[None]), 0.0
    )
    query_decay = jnp.exp(-decays[None, :] * (offsets[:, None] + 1.0))
    key_decay = jnp.exp(-decays[None, :] * (length - 1.0 - offsets[:, None]))
    per_block = jnp.exp(-decays * length)
    return (within, query_decay, key_decay, per_block)


def dot(left, right, contract):
    return lax.dot_general(left, right, (contract, ((), ())), preferred_element_type=f32)


def solution(mesh):
    groups = Groups(mesh)
    fine = Mesh(
        mesh.devices.reshape(-1, CORES, mesh.shape["sp"]),
        ALL,
    )
    members = groups.models
    teams = groups.tokens
    heads_dev = HEADS // members
    own_keys = heads_dev * KEY
    own_values = heads_dev * VAL
    units = FF // members
    key_scale = KEY ** (-0.5)

    def state_prefix(last, decay, backward):
        own = last.astype(bf16)
        total = jnp.zeros(last.shape, f32)
        weight = jnp.ones_like(decay)
        for step in range(1, teams):
            pairs = [(i, i + step) for i in range(teams - step)]
            if backward:
                pairs = [(b, a) for a, b in pairs]
            got = lax.ppermute(own, groups.token, pairs)
            total = total + weight[:, None, None] * got.astype(f32)
            weight = weight * decay
        return total

    def on_device(
        block_input,
        out_grad,
        qkvg_weight,
        out_weight,
        mlp_in_weight,
        mlp_out_weight,
        norm_gains,
        group_gain,
        decay_rate,
    ):
        member = lax.axis_index(groups.model)
        rows = block_input.shape[0]
        weight_rows = qkvg_weight.shape[0]
        key_cols = HEADS * KEY
        value_cols = HEADS * VAL
        decays = lax.dynamic_slice_in_dim(decay_rate, member * heads_dev, heads_dev)

        def by_member(columns):
            return columns.reshape(weight_rows, members, -1).transpose(1, 0, 2)

        qkvg_blocks = jnp.concatenate(
            [
                by_member(qkvg_weight[:, :key_cols]),
                by_member(qkvg_weight[:, key_cols : 2 * key_cols]),
                by_member(qkvg_weight[:, 2 * key_cols : 2 * key_cols + value_cols]),
                by_member(qkvg_weight[:, 2 * key_cols + value_cols :]),
            ],
            axis=2,
        )
        own_cols = qkvg_blocks.shape[2]
        own_qkvg = groups.gather_token(groups.exchange(qkvg_blocks).reshape(-1, own_cols))
        unit_block = mlp_out_weight.shape[0]
        in_blocks = (
            mlp_in_weight.reshape(weight_rows, 2, teams, members, unit_block)
            .transpose(3, 0, 1, 2, 4)
            .reshape(members, weight_rows, 2 * units)
        )
        own_out = groups.gather_token(lax.ppermute(out_weight, ALL, groups.owner_pairs()))
        own_in = groups.gather_token(groups.exchange(in_blocks).reshape(-1, 2 * units))
        own_down = groups.gather_token(mlp_out_weight)

        full_gains = lax.all_gather(norm_gains, ALL, axis=1, tiled=True)
        full_group = lax.all_gather(group_gain, ALL, axis=0, tiled=True)
        gain_one = full_gains[0].astype(f32)
        gain_two = full_gains[1].astype(f32)
        gain_group = lax.dynamic_slice_in_dim(
            full_group.astype(f32), member * own_values, own_values
        )

        normed_one, inv_one = layer_norm(block_input)
        hidden_one = (normed_one * gain_one).astype(bf16)
        hidden_rows = groups.gather_model(hidden_one)
        own_proj = dot(hidden_rows, own_qkvg, ((1,), (0,)))
        query_rows = (own_proj[:, :own_keys] * key_scale).astype(bf16)
        key_rows = own_proj[:, own_keys : 2 * own_keys].astype(bf16)
        value_rows = own_proj[:, 2 * own_keys : 2 * own_keys + own_values].astype(bf16)
        gate_values = own_proj[:, 2 * own_keys + own_values :]
        rows_here = rows * members
        block_count = rows_here // BLOCK
        within, query_decay, key_decay, per_block = decay_tables(decays, BLOCK)
        query_blocks = query_rows.reshape(block_count, BLOCK, heads_dev, KEY)
        key_blocks = key_rows.reshape(block_count, BLOCK, heads_dev, KEY)
        value_blocks = value_rows.reshape(block_count, BLOCK, heads_dev, VAL)
        query_scaled = (query_blocks * query_decay[None, :, :, None]).astype(bf16)
        key_scaled = (key_blocks * key_decay[None, :, :, None]).astype(bf16)
        updates = jnp.einsum(
            "nihk,nihv->nhkv", key_scaled, value_blocks, preferred_element_type=f32
        )
        zero_state = jnp.zeros((heads_dev, KEY, VAL), f32)
        block_decay = jnp.exp(-decays * rows_here)

        running = zero_state
        local_prior = []
        for index in range(block_count):
            local_prior.append(running)
            running = per_block[:, None, None] * running + updates[index]
        incoming = state_prefix(running, block_decay, False)
        scores = (
            jnp.einsum("nihk,njhk->nhij", query_blocks, key_blocks, preferred_element_type=f32)
            * within[None]
        ).astype(bf16)
        intra_part = jnp.einsum(
            "nhij,njhv->nihv", scores, value_blocks, preferred_element_type=f32
        )
        state_rounded = jnp.stack(
            [
                prior + jnp.exp(-decays * (BLOCK * index))[:, None, None] * incoming
                for index, prior in enumerate(local_prior)
            ]
        ).astype(bf16)
        retained = intra_part + jnp.einsum(
            "nihk,nhkv->nihv", query_scaled, state_rounded, preferred_element_type=f32
        )
        group_normed, group_inv = layer_norm(retained.reshape(rows_here, heads_dev, VAL))
        group_tok = group_normed.astype(bf16).astype(f32).reshape(rows_here, own_values)
        sigmoid_gate = jax.nn.sigmoid(gate_values)
        swish_gate = gate_values * sigmoid_gate
        mixed_own = (gain_group * group_tok * swish_gate).astype(bf16)

        def out_part(first, count):
            piece = lax.dynamic_slice_in_dim(mixed_own, first, count)
            return dot(piece, own_out, ((1,), (0,)))

        middle = block_input + groups.scatter_model(out_part, rows)
        normed_two, inv_two = layer_norm(middle)
        hidden_two = (normed_two * gain_two).astype(bf16)
        out_rows = groups.gather_model(out_grad.astype(bf16))
        mid_rows = groups.gather_model(hidden_two)
        inner_own = dot(mid_rows, own_in, ((1,), (0,)))
        activated, gelu_slope = gelu_parts(inner_own[:, :units])
        up_part = inner_own[:, units:]
        product = (activated * up_part).astype(bf16)
        grad_product = dot(out_rows, own_down, ((1,), (1,)))
        grad_inner = jnp.concatenate(
            [grad_product * up_part * gelu_slope, grad_product * activated], axis=1
        ).astype(bf16)

        def grad_two_part(first, count):
            piece = lax.dynamic_slice_in_dim(grad_inner, first, count)
            return dot(piece, own_in, ((1,), (1,)))

        grad_hidden_two = groups.scatter_model(grad_two_part, rows)
        gain_two_term = jnp.sum(grad_hidden_two * normed_two, axis=0)
        grad_middle = out_grad + norm_back(grad_hidden_two * gain_two, normed_two, inv_two)
        middle_rows = groups.gather_model(grad_middle.astype(bf16))

        def down_part(first, count):
            piece = lax.dynamic_slice_in_dim(product, first, count)
            return dot(piece, own_down, ((1,), (0,)))

        block_output = middle + groups.scatter_model(down_part, rows)
        down_term = dot(product, out_rows, ((0,), (0,))).astype(bf16)
        down_grad_dev = groups.scatter_token(down_term).astype(f32)
        in_term = dot(mid_rows, grad_inner, ((0,), (0,))).astype(bf16)
        in_piece = groups.scatter_token(in_term)

        mixed_grad_own = dot(middle_rows, own_out, ((1,), (1,)))
        out_term = dot(mixed_own, middle_rows, ((0,), (0,))).astype(bf16)
        out_piece = groups.scatter_token(out_term)
        out_grad_dev = lax.ppermute(
            out_piece, ALL, [(b, a) for a, b in groups.owner_pairs()]
        ).astype(f32)
        own_group_term = jnp.sum(mixed_grad_own * group_tok * swish_gate, axis=0)
        grad_group_rows = (
            (mixed_grad_own * gain_group * swish_gate)
            .astype(bf16)
            .astype(f32)
            .reshape(rows_here, heads_dev, VAL)
        )
        grad_gate = (
            mixed_grad_own
            * gain_group
            * group_tok
            * sigmoid_gate
            * (1.0 + gate_values * (1.0 - sigmoid_gate))
        )
        grad_retained = (
            norm_back(grad_group_rows, group_normed, group_inv)
            .astype(bf16)
            .reshape(block_count, BLOCK, heads_dev, VAL)
        )
        directs = jnp.einsum(
            "nihk,nihv->nhkv", query_scaled, grad_retained, preferred_element_type=f32
        )
        running = zero_state
        later_local = [None] * block_count
        for index in reversed(range(block_count)):
            later_local[index] = running
            running = per_block[:, None, None] * running + directs[index]
        returned = state_prefix(running, block_decay, True)
        grad_scores = (
            jnp.einsum(
                "nihv,njhv->nhij", grad_retained, value_blocks, preferred_element_type=f32
            )
            * within[None]
        ).astype(bf16)
        later_rounded = jnp.stack(
            [
                later + jnp.exp(-decays * (BLOCK * (block_count - 1 - index)))[:, None, None] * returned
                for index, later in enumerate(later_local)
            ]
        ).astype(bf16)
        grad_query = (
            jnp.einsum("nhij,njhk->nihk", grad_scores, key_blocks, preferred_element_type=f32)
            + jnp.einsum(
                "nihv,nhkv->nihk", grad_retained, state_rounded, preferred_element_type=f32
            )
            * query_decay[None, :, :, None]
        ) * key_scale
        grad_key = (
            jnp.einsum("nhij,nihk->njhk", grad_scores, query_blocks, preferred_element_type=f32)
            + jnp.einsum(
                "nihv,nhkv->nihk", value_blocks, later_rounded, preferred_element_type=f32
            )
            * key_decay[None, :, :, None]
        )
        grad_value = jnp.einsum(
            "nhij,nihv->njhv", scores, grad_retained, preferred_element_type=f32
        ) + jnp.einsum("nihk,nhkv->nihv", key_scaled, later_rounded, preferred_element_type=f32)
        grad_projected = jnp.concatenate(
            [
                grad_query.astype(bf16).reshape(rows_here, own_keys),
                grad_key.astype(bf16).reshape(rows_here, own_keys),
                grad_value.astype(bf16).reshape(rows_here, own_values),
                grad_gate.astype(bf16),
            ],
            axis=1,
        )
        qkvg_term = dot(hidden_rows, grad_projected, ((0,), (0,))).astype(bf16)
        column_piece = groups.scatter_token(qkvg_term)

        def grad_one_part(first, count):
            piece = lax.dynamic_slice_in_dim(grad_projected, first, count)
            return dot(piece, own_qkvg, ((1,), (1,)))

        grad_hidden_one = groups.scatter_model(grad_one_part, rows)
        gain_one_term = jnp.sum(grad_hidden_one * normed_one, axis=0)
        input_grad = grad_middle + norm_back(grad_hidden_one * gain_one, normed_one, inv_one)

        gains_grad = lax.psum_scatter(
            jnp.stack([gain_one_term, gain_two_term]), ALL, scatter_dimension=1, tiled=True
        )
        group_term = lax.dynamic_update_slice_in_dim(
            jnp.zeros((value_cols,), f32), own_group_term, member * own_values, 0
        )
        group_grad = lax.psum_scatter(group_term, ALL, scatter_dimension=0, tiled=True)

        in_home = groups.exchange(in_piece.reshape(members, weight_rows, 2 * units))
        in_grad_dev = (
            in_home.astype(f32)
            .reshape(members, weight_rows, 2, teams, unit_block)
            .transpose(1, 2, 3, 0, 4)
            .reshape(weight_rows, 2 * FF)
        )
        home = groups.exchange(column_piece.reshape(members, weight_rows, own_cols))
        home = home.astype(f32).transpose(1, 0, 2)
        cuts = (0, own_keys, 2 * own_keys, 2 * own_keys + own_values, own_cols)
        qkvg_grad = jnp.concatenate(
            [home[:, :, a:b].reshape(weight_rows, -1) for a, b in zip(cuts, cuts[1:])], axis=1
        )
        return (
            block_output,
            input_grad,
            qkvg_grad,
            out_grad_dev,
            in_grad_dev,
            down_grad_dev,
            gains_grad,
            group_grad,
        )

    return jax.shard_map(
        on_device,
        mesh=fine,
        in_specs=(
            P(ALL, None),
            P(ALL, None),
            P(ALL, None),
            P(ALL, None),
            P(ALL, None),
            P(ALL, None),
            P(None, ALL),
            P(ALL),
            P(),
        ),
        out_specs=(
            P(ALL, None),
            P(ALL, None),
            P(ALL, None),
            P(ALL, None),
            P(ALL, None),
            P(ALL, None),
            P(None, ALL),
            P(ALL),
        ),
        check_vma=False,
    )
```

```python
import functools
import math

import jax
import jax.numpy as jnp
from jax import lax
from jax.experimental import pallas as pl
from jax.experimental.pallas import tpu as pltpu
from jax.sharding import Mesh, PartitionSpec as P

D = 2048
HEADS = 8
KEY = 256
VAL = 512
FF = 4096
SEQS = 1
BLOCK = 512

epsilon = 1e-05
CORES = 2
ALL = ("chip", "core", "sp")
bf16 = jnp.bfloat16
f32 = jnp.float32


def layer_norm(values):
    average = jnp.mean(values, axis=-1, keepdims=True)
    centered = values - average
    inv_std = lax.rsqrt(jnp.mean(centered * centered, axis=-1, keepdims=True) + epsilon)
    return (centered * inv_std, inv_std)


def norm_back(upstream, normed, inv_std):
    return inv_std * (
        upstream
        - jnp.mean(upstream, axis=-1, keepdims=True)
        - normed * jnp.mean(upstream * normed, axis=-1, keepdims=True)
    )


def gelu_parts(inputs):
    normal_cdf = 0.5 * (1.0 + lax.erf(inputs * 0.7071067811865476))
    return (
        inputs * normal_cdf,
        normal_cdf + inputs * jnp.exp(-0.5 * inputs * inputs) * 0.3989422804014327,
    )


def shift(value, axis, step):
    count = lax.axis_size(axis)
    return lax.ppermute(value, axis, [(i, (i + step) % count) for i in range(count)])


def flip(value, axis, bit):
    count = lax.axis_size(axis)
    return lax.ppermute(value, axis, [(i, i ^ bit) for i in range(count)])


def take(buffer, index):
    return lax.dynamic_index_in_dim(buffer, index, 0, False)


def place_pieces(sizes, order_ref, *refs):
    pieces, target, sems = refs[: len(sizes)], refs[len(sizes)], refs[len(sizes) + 1]
    copies = []
    for piece, size in zip(pieces, sizes):
        for i in range(size):
            n = len(copies)
            copies.append(
                pltpu.make_async_copy(piece.at[i], target.at[order_ref[n]], sems.at[n])
            )
    for copy in copies:
        copy.start()
    for copy in copies:
        copy.wait()


def place(pieces, order):
    sizes = tuple(piece.shape[0] for piece in pieces)
    count = sum(sizes)
    shape = (count,) + pieces[0].shape[1:]
    size = math.prod(shape) * pieces[0].dtype.itemsize
    return pl.pallas_call(
        functools.partial(place_pieces, sizes),
        out_shape=jax.ShapeDtypeStruct(shape, pieces[0].dtype),
        in_specs=[pl.BlockSpec(memory_space=pltpu.SMEM)]
        + [pl.BlockSpec(memory_space=pl.ANY)] * len(pieces),
        out_specs=pl.BlockSpec(memory_space=pltpu.VMEM),
        scratch_shapes=[pltpu.SemaphoreType.DMA((count,))],
        compiler_params=pltpu.CompilerParams(vmem_limit_bytes=size + (4 << 20)),
        cost_estimate=pl.CostEstimate(flops=0, bytes_accessed=2 * size, transcendentals=0),
    )(order.astype(jnp.int32), *pieces)


class Groups:
    def __init__(self, mesh):
        count = mesh.shape["sp"]
        self.split = HEADS % (CORES * count) == 0 and mesh.size == 4 * CORES * count
        self.model = ("core", "sp") if self.split else ("sp",)
        self.token = ("chip",) if self.split else ("chip", "core")
        self.sp = count
        self.models = count * (CORES if self.split else 1)
        self.tokens = mesh.size // self.models

    def gather_model(self, value):
        return self.finish_gather(self.start_gather(value))

    def start_gather(self, value):
        if not self.split:
            return [lax.all_gather(value, self.model, axis=0, tiled=True)]
        return [value] + [shift(value, "sp", step) for step in range(1, self.sp)]

    def finish_gather(self, own):
        if not self.split:
            return own[0]
        return jnp.concatenate(own + [flip(got, "core", 1) for got in own], axis=0)

    def scatter_model(self, part_of, rows, wait=None):
        if not self.split:
            whole = part_of(0, rows * self.models)
            return lax.psum_scatter(
                whole.astype(bf16), self.model, scatter_dimension=0, tiled=True
            ).astype(f32)
        half = rows * self.sp
        came = flip(part_of(half, half).astype(bf16), "core", 1)
        own = part_of(0, half) + came.astype(f32)
        total = own[:rows]
        low = own.astype(bf16)
        if wait is not None:
            low = after(low, wait)
        for step in range(1, self.sp):
            got = shift(low[step * rows : (step + 1) * rows], "sp", -step)
            total = total + got.astype(f32)
        return total

    def token_pieces(self, value):
        return [value] + [flip(value, "chip", bit) for bit in range(1, self.tokens)]

    def gather_token(self, value):
        if not self.split:
            return lax.all_gather(value, self.token, axis=0, tiled=True)
        half = value.shape[0] // 2
        near = flip(value, "chip", 1)
        far = flip(value, "chip", 2)
        return jnp.concatenate(
            [value, near, far, flip(far[:half], "chip", 1), flip(near[half:], "chip", 2)], axis=0
        )

    def gather_token_direct(self, value):
        if not self.split:
            return lax.all_gather(value, self.token, axis=0, tiled=True)
        return jnp.concatenate(self.token_pieces(value), axis=0)

    def gather_token_natural(self, value):
        if not self.split:
            return lax.all_gather(value, self.token, axis=0, tiled=True)
        pieces = [piece[None] for piece in self.token_pieces(value)]
        return place(pieces, self.chip_order()).reshape((-1,) + value.shape[1:])

    def scatter_token(self, value):
        if not self.split:
            return lax.psum_scatter(value, self.token, scatter_dimension=0, tiled=True).astype(f32)
        rows = value.shape[0] // 4
        half = rows // 2
        own, near, far, cross = (value[i * rows : (i + 1) * rows] for i in range(4))
        to_far = flip(cross[:half], "chip", 1)
        to_near = flip(cross[half:], "chip", 2)
        near = jnp.concatenate([near[:half], near[half:] + to_near])
        far = jnp.concatenate([far[:half] + to_far, far[half:]])
        got = flip(near, "chip", 1).astype(f32) + flip(far, "chip", 2).astype(f32)
        return own.astype(f32) + got

    def chip_order(self):
        return jnp.arange(self.tokens) ^ lax.axis_index("chip")

    def own_order(self, value):
        if not self.split:
            return value
        blocks = value.reshape((self.tokens, -1) + value.shape[1:])
        order = self.chip_order()
        return jnp.concatenate([take(blocks, order[i]) for i in range(self.tokens)], axis=0)

    def columns(self, value):
        if not self.split:
            return value
        chip = lax.axis_index("chip")
        width = value.shape[1] // self.tokens
        return jnp.concatenate(
            [
                lax.dynamic_slice_in_dim(value, (chip ^ i) * width, width, 1)
                for i in range(self.tokens)
            ],
            axis=1,
        )

    def exchange(self, blocks, wait=None):
        if not self.split:
            return lax.all_to_all(blocks, self.model, split_axis=0, concat_axis=0, tiled=True)
        place_sp = lax.axis_index("sp")
        core = lax.axis_index("core")
        halves = blocks.reshape((CORES, self.sp) + blocks.shape[1:])
        pair = jnp.stack([take(halves, core), flip(take(halves, 1 - core), "core", 1)], axis=1)
        if wait is not None:
            pair = after(pair, wait)
        came = [take(pair, place_sp)]
        for step in range(1, self.sp):
            came.append(shift(take(pair, (place_sp + step) % self.sp), "sp", step))
        index = jnp.arange(self.models)
        order = (index % CORES + core) % CORES * self.sp + (place_sp - index // CORES) % self.sp
        return came, order

    def settle(self, came):
        if not self.split:
            return came
        return place(*came)

    def owner_pairs(self):
        return [
            (d, (d % self.tokens) * self.models + d // self.tokens)
            for d in range(self.tokens * self.models)
        ]

    def gather_small(self, value):
        if not self.split:
            return lax.all_gather(value, ALL)
        place = lax.axis_index("sp")
        core = lax.axis_index("core")
        got = jnp.stack([value] + [shift(value, "sp", step) for step in range(1, self.sp)])
        got = jnp.take(got, (place - jnp.arange(self.sp)) % self.sp, axis=0)
        both = jnp.stack([got, flip(got, "core", 1)])
        both = jnp.take(both, (core + jnp.arange(CORES)) % CORES, axis=0)
        whole = jnp.stack([both] + [flip(both, "chip", bit) for bit in range(1, self.tokens)])
        return jnp.take(whole, self.chip_order(), axis=0).reshape(-1, value.shape[0])

    def scatter_small(self, value):
        if not self.split:
            return lax.psum_scatter(value, ALL, scatter_dimension=0)
        place = lax.axis_index("sp")
        core = lax.axis_index("core")
        value = value.reshape(self.tokens, CORES, self.sp, -1).transpose(2, 0, 1, 3)
        value = jnp.take(value, (place + jnp.arange(self.sp)) % self.sp, axis=0)
        value = value[0] + sum(shift(value[step], "sp", step) for step in range(1, self.sp))
        value = jnp.take(value, (core + jnp.arange(CORES)) % CORES, axis=1)
        value = value[:, 0] + flip(value[:, 1], "core", 1)
        value = jnp.take(value, self.chip_order(), axis=0)
        return value[0] + sum(flip(value[bit], "chip", bit) for bit in range(1, self.tokens))


def decay_tables(decays, place, length):
    spread = place[:, None] - place[None, :]
    within = jnp.where(
        spread[None] >= 0.0, jnp.exp(-decays[:, None, None] * jnp.maximum(spread, 0.0)[None]), 0.0
    )
    query_decay = jnp.exp(-decays[None, :] * (place[:, None] + 1.0))
    key_decay = jnp.exp(-decays[None, :] * (length - 1.0 - place[:, None]))
    per_block = jnp.exp(-decays * length)
    return (within, query_decay, key_decay, per_block)


def dot(left, right, contract):
    return lax.dot_general(left, right, (contract, ((), ())), preferred_element_type=f32)


def after(value, *others):
    return lax.optimization_barrier((value,) + others)[0]


def solution(mesh):
    groups = Groups(mesh)
    fine = Mesh(
        mesh.devices.reshape(-1, CORES, mesh.shape["sp"]),
        ALL,
    )
    members = groups.models
    teams = groups.tokens
    heads_dev = HEADS // members
    own_keys = heads_dev * KEY
    own_values = heads_dev * VAL
    units = FF // members
    key_scale = KEY ** (-0.5)

    def state_prefix(last, decay, backward):
        own = last.astype(bf16)
        total = jnp.zeros(last.shape, f32)
        weight = jnp.ones_like(decay)
        for step in range(1, teams):
            pairs = [(i, i + step) for i in range(teams - step)]
            if backward:
                pairs = [(b, a) for a, b in pairs]
            got = lax.ppermute(own, groups.token, pairs)
            total = total + weight[:, None, None] * got.astype(f32)
            weight = weight * decay
        return total

    def chain(updates, per_block, incoming, swapped):
        if swapped is None:
            before = []
            running = incoming
            for update in updates:
                before.append(running)
                running = per_block[:, None, None] * running + update
            return before, running
        rate = per_block[:, None, None]
        after_zero = rate * incoming + updates[0]
        after_one = rate * incoming + updates[1]
        before = [
            jnp.where(swapped, after_one, incoming),
            jnp.where(swapped, incoming, after_zero),
        ]
        last = jnp.where(swapped, rate * after_one + updates[0], rate * after_zero + updates[1])
        return before, last

    def on_device(
        block_input,
        out_grad,
        qkvg_weight,
        out_weight,
        mlp_in_weight,
        mlp_out_weight,
        norm_gains,
        group_gain,
        decay_rate,
    ):
        member = lax.axis_index(groups.model)
        rows = block_input.shape[0]
        weight_rows = qkvg_weight.shape[0]
        unit_block = mlp_out_weight.shape[0]
        key_cols = HEADS * KEY
        value_cols = HEADS * VAL
        decays = lax.dynamic_slice_in_dim(decay_rate, member * heads_dev, heads_dev)
        rows_here = rows * members
        if groups.split:
            length = rows * groups.sp
            place = jnp.arange(length) // rows
            place = (lax.axis_index("sp") - place) % groups.sp * rows + jnp.arange(length) % rows
            swapped = lax.axis_index("core") == 1
        else:
            length = BLOCK
            place = jnp.arange(length)
            swapped = None
        block_count = rows_here // length

        def by_member(columns):
            return columns.reshape(weight_rows, members, -1).transpose(1, 0, 2)

        small = groups.gather_small(
            jnp.concatenate([norm_gains.reshape(-1), group_gain], axis=0)
        ).astype(f32)
        gain_cols = norm_gains.shape[1]
        gain_one = small[:, :gain_cols].reshape(-1)
        gain_two = small[:, gain_cols : 2 * gain_cols].reshape(-1)
        gain_group = lax.dynamic_slice_in_dim(
            small[:, 2 * gain_cols :].reshape(-1), member * own_values, own_values
        )
        qkvg_blocks = jnp.concatenate(
            [
                by_member(qkvg_weight[:, :key_cols]),
                by_member(qkvg_weight[:, key_cols : 2 * key_cols]),
                by_member(qkvg_weight[:, 2 * key_cols : 2 * key_cols + value_cols]),
                by_member(qkvg_weight[:, 2 * key_cols + value_cols :]),
            ],
            axis=2,
        )
        own_cols = qkvg_blocks.shape[2]
        qkvg_sent = groups.exchange(qkvg_blocks)
        qkvg_came = groups.settle(qkvg_sent).reshape(-1, own_cols)
        own_qkvg = groups.gather_token(qkvg_came)
        own_down = groups.gather_token_natural(mlp_out_weight)

        out_came = lax.ppermute(after(out_weight, qkvg_came), ALL, groups.owner_pairs())
        normed_one, inv_one = layer_norm(block_input)
        hidden_one = (normed_one * gain_one).astype(bf16)
        hidden_rows = groups.gather_model(after(groups.columns(hidden_one), qkvg_came))
        own_out = groups.gather_token_natural(after(out_came, own_qkvg))

        in_blocks = (
            mlp_in_weight.reshape(weight_rows, 2, teams, members, unit_block)
            .transpose(3, 0, 1, 2, 4)
            .reshape(members, weight_rows, 2 * units)
        )
        in_sent = groups.exchange(in_blocks, hidden_rows)
        out_started = groups.start_gather(after(out_grad.astype(bf16), hidden_rows))

        own_proj = dot(hidden_rows, own_qkvg, ((1,), (0,)))
        query_rows = (own_proj[:, :own_keys] * key_scale).astype(bf16)
        key_rows = own_proj[:, own_keys : 2 * own_keys].astype(bf16)
        value_rows = own_proj[:, 2 * own_keys : 2 * own_keys + own_values].astype(bf16)
        gate_values = own_proj[:, 2 * own_keys + own_values :]
        within, query_decay, key_decay, per_block = decay_tables(
            decays, place.astype(f32), length
        )
        query_blocks = query_rows.reshape(block_count, length, heads_dev, KEY)
        key_blocks = key_rows.reshape(block_count, length, heads_dev, KEY)
        value_blocks = value_rows.reshape(block_count, length, heads_dev, VAL)
        query_scaled = (query_blocks * query_decay[None, :, :, None]).astype(bf16)
        key_scaled = (key_blocks * key_decay[None, :, :, None]).astype(bf16)
        updates = jnp.einsum(
            "nihk,nihv->nhkv", key_scaled, value_blocks, preferred_element_type=f32
        )
        zero_state = jnp.zeros((heads_dev, KEY, VAL), f32)
        block_decay = jnp.exp(-decays * rows_here)

        _, local_last = chain(updates, per_block, zero_state, swapped)
        incoming = state_prefix(local_last, block_decay, False)
        scores = (
            jnp.einsum("nihk,njhk->nhij", query_blocks, key_blocks, preferred_element_type=f32)
            * within[None]
        ).astype(bf16)
        intra_part = jnp.einsum(
            "nhij,njhv->nihv", scores, value_blocks, preferred_element_type=f32
        )
        prior, _ = chain(updates, per_block, incoming, swapped)
        state_rounded = jnp.stack(prior).astype(bf16)
        retained = intra_part + jnp.einsum(
            "nihk,nhkv->nihv", query_scaled, state_rounded, preferred_element_type=f32
        )
        group_normed, group_inv = layer_norm(retained.reshape(rows_here, heads_dev, VAL))
        group_tok = group_normed.astype(bf16).astype(f32).reshape(rows_here, own_values)
        sigmoid_gate = jax.nn.sigmoid(gate_values)
        swish_gate = gate_values * sigmoid_gate
        mixed_own = (gain_group * group_tok * swish_gate).astype(bf16)

        mixed_own, own_out, out_started, in_sent = lax.optimization_barrier(
            (mixed_own, own_out, out_started, in_sent)
        )

        def out_part(first, count):
            return dot(mixed_own[first : first + count], own_out, ((1,), (0,)))

        middle = block_input + groups.scatter_model(out_part, rows)
        normed_two, inv_two = layer_norm(middle)
        hidden_two = (normed_two * gain_two).astype(bf16)
        own_in = groups.gather_token_direct(
            groups.settle(in_sent).reshape(-1, 2 * units)
        )
        out_rows = groups.finish_gather(out_started)
        mid_rows = groups.gather_model(groups.columns(hidden_two))
        inner_own = dot(mid_rows, own_in, ((1,), (0,)))
        activated, gelu_slope = gelu_parts(inner_own[:, :units])
        up_part = inner_own[:, units:]
        product = (activated * up_part).astype(bf16)
        grad_product = dot(out_rows, own_down, ((1,), (1,)))
        grad_inner = jnp.concatenate(
            [grad_product * up_part * gelu_slope, grad_product * activated], axis=1
        ).astype(bf16)

        def grad_two_part(first, count):
            return dot(grad_inner[first : first + count], own_in, ((1,), (1,)))

        grad_hidden_two = groups.columns(groups.scatter_model(grad_two_part, rows))
        gain_two_term = jnp.sum(grad_hidden_two * normed_two, axis=0)
        grad_middle = out_grad + norm_back(grad_hidden_two * gain_two, normed_two, inv_two)
        middle_rows = groups.gather_model(grad_middle.astype(bf16))

        down_term = dot(product, out_rows, ((0,), (0,))).astype(bf16)
        down_grad_dev = groups.scatter_token(groups.own_order(down_term))
        in_term = dot(mid_rows, grad_inner, ((0,), (0,))).astype(bf16)
        in_piece = groups.scatter_token(in_term).astype(bf16)
        in_home = groups.exchange(
            in_piece.reshape(members, weight_rows, 2 * units), middle_rows
        )

        def down_part(first, count):
            return dot(product[first : first + count], own_down, ((1,), (0,)))

        mlp_sum = groups.scatter_model(down_part, rows, middle_rows)

        mixed_grad_own = dot(middle_rows, own_out, ((1,), (1,)))
        out_term = dot(mixed_own, middle_rows, ((0,), (0,))).astype(bf16)
        out_piece = groups.scatter_token(groups.own_order(out_term)).astype(bf16)
        own_group_term = jnp.sum(mixed_grad_own * group_tok * swish_gate, axis=0)
        grad_group_rows = (
            (mixed_grad_own * gain_group * swish_gate)
            .astype(bf16)
            .astype(f32)
            .reshape(rows_here, heads_dev, VAL)
        )
        grad_gate = (
            mixed_grad_own
            * gain_group
            * group_tok
            * sigmoid_gate
            * (1.0 + gate_values * (1.0 - sigmoid_gate))
        )
        grad_retained = (
            norm_back(grad_group_rows, group_normed, group_inv)
            .astype(bf16)
            .reshape(block_count, length, heads_dev, VAL)
        )
        directs = jnp.einsum(
            "nihk,nihv->nhkv", query_scaled, grad_retained, preferred_element_type=f32
        )
        turned = None if swapped is None else swapped
        _, own_total = chain(directs[::-1], per_block, zero_state, turned)
        returned = state_prefix(own_total, block_decay, True)
        grad_scores = (
            jnp.einsum(
                "nihv,njhv->nhij", grad_retained, value_blocks, preferred_element_type=f32
            )
            * within[None]
        ).astype(bf16)
        later, _ = chain(directs[::-1], per_block, returned, turned)
        later_rounded = jnp.stack(later[::-1]).astype(bf16)
        grad_query = (
            jnp.einsum("nhij,njhk->nihk", grad_scores, key_blocks, preferred_element_type=f32)
            + jnp.einsum(
                "nihv,nhkv->nihk", grad_retained, state_rounded, preferred_element_type=f32
            )
            * query_decay[None, :, :, None]
        ) * key_scale
        grad_key = (
            jnp.einsum("nhij,nihk->njhk", grad_scores, query_blocks, preferred_element_type=f32)
            + jnp.einsum(
                "nihv,nhkv->nihk", value_blocks, later_rounded, preferred_element_type=f32
            )
            * key_decay[None, :, :, None]
        )
        grad_value = jnp.einsum(
            "nhij,nihv->njhv", scores, grad_retained, preferred_element_type=f32
        ) + jnp.einsum("nihk,nhkv->nihv", key_scaled, later_rounded, preferred_element_type=f32)
        grad_projected = jnp.concatenate(
            [
                grad_query.astype(bf16).reshape(rows_here, own_keys),
                grad_key.astype(bf16).reshape(rows_here, own_keys),
                grad_value.astype(bf16).reshape(rows_here, own_values),
                grad_gate.astype(bf16),
            ],
            axis=1,
        )
        grad_projected, mlp_sum, in_home = lax.optimization_barrier(
            (grad_projected, mlp_sum, in_home)
        )
        block_output = middle + mlp_sum
        qkvg_term = dot(hidden_rows, grad_projected, ((0,), (0,))).astype(bf16)
        column_piece = groups.scatter_token(qkvg_term).astype(bf16)

        def grad_one_part(first, count):
            return dot(grad_projected[first : first + count], own_qkvg, ((1,), (1,)))

        grad_hidden_one = groups.columns(groups.scatter_model(grad_one_part, rows))
        gain_one_term = jnp.sum(grad_hidden_one * normed_one, axis=0)
        input_grad = grad_middle + norm_back(grad_hidden_one * gain_one, normed_one, inv_one)

        group_term = lax.dynamic_update_slice_in_dim(
            jnp.zeros((value_cols,), f32), own_group_term, member * own_values, 0
        )
        devices = teams * members
        small_grad = groups.scatter_small(
            jnp.concatenate(
                [
                    gain_one_term.reshape(devices, -1),
                    gain_two_term.reshape(devices, -1),
                    group_term.reshape(devices, -1),
                ],
                axis=1,
            )
        ).reshape(-1)
        gains_grad = small_grad[: 2 * gain_cols].reshape(2, gain_cols)
        group_grad = small_grad[2 * gain_cols :]

        out_grad_dev = lax.ppermute(
            out_piece, ALL, [(b, a) for a, b in groups.owner_pairs()]
        ).astype(f32)
        in_home = groups.settle(in_home)
        in_grad_dev = (
            in_home.astype(f32)
            .reshape(members, weight_rows, 2, teams, unit_block)
            .transpose(1, 2, 3, 0, 4)
            .reshape(weight_rows, 2 * FF)
        )
        home = groups.settle(
            groups.exchange(column_piece.reshape(members, weight_rows, own_cols))
        )
        home = home.astype(f32).transpose(1, 0, 2)
        cuts = (0, own_keys, 2 * own_keys, 2 * own_keys + own_values, own_cols)
        qkvg_grad = jnp.concatenate(
            [home[:, :, a:b].reshape(weight_rows, -1) for a, b in zip(cuts, cuts[1:])], axis=1
        )
        return (
            block_output,
            input_grad,
            qkvg_grad,
            out_grad_dev,
            in_grad_dev,
            down_grad_dev,
            gains_grad,
            group_grad,
        )

    return jax.shard_map(
        on_device,
        mesh=fine,
        in_specs=(
            P(ALL, None),
            P(ALL, None),
            P(ALL, None),
            P(ALL, None),
            P(ALL, None),
            P(ALL, None),
            P(None, ALL),
            P(ALL),
            P(),
        ),
        out_specs=(
            P(ALL, None),
            P(ALL, None),
            P(ALL, None),
            P(ALL, None),
            P(ALL, None),
            P(ALL, None),
            P(None, ALL),
            P(ALL),
        ),
        check_vma=False,
    )
```
